32 devices in a mesh: strip: 4 (over y, x), depth: 8 (over z, core).
Axes of the slice: x: 2, y: 2, z: 4, core: 2. Of those that a mesh axis runs over, the one named last changes fastest.
Arguments:
- volume: bfloat16 [64, 128, 2048], P('depth', 'strip'), may hold values from -6 to 6
- occupancy: int32 [8, 4, 16], P('depth', 'strip'), may hold values from 0 to 1
- slab_order: int32 [8], replicated, may hold values from 0 to 7, as said below
- w_in: bfloat16 [4, 64], replicated, may hold values from -3 to 3
- b_in: float32 [64], replicated, may hold values from -3 to 3
- w_out: bfloat16 [64, 4], replicated, may hold values from -1.5 to 1.5
- b_out: float32 [4], replicated, may hold values from -3 to 3
- conv_weight: float32 [3, 3, 3, 3], replicated, may hold values from -1.25 to 1.25
- conv_bias: float32 [3], replicated, may hold values from -3 to 3
Outputs:
- denoised: float32 [3, 4, 4, 8, 2048], P(None, 'strip', None, 'depth')
The draws below stay inside these ranges and needn't reach their ends.
Inputs may be any that keep to these rules, and one draw needn't show every extreme that they name: slab_order is a permutation; for every bit b, bit b of slab_order[d] is bit b of d XOR a value that depends only on d's bits above b (so slabs that agree on their bits above b hold consecutive positions).
All inputs are finite; a program needn't handle non-finite values.
Results may differ from the reference program's by a relative error of at most 0.0003.
Values may be sent and summed in bfloat16 or wider, within the bound.
A program may use at most 64 MiB of HBM per device.

```python
import jax
import jax.numpy as jnp
from jax import lax

WIDTH = 2048
Z_DEV = 8
CHANNELS = 4
HIDDEN_SIZE = 64
BRICK_ROWS = 32
BRICK_COLS = 128
HEIGHT = 128
DEPTH = 64
ROW_SHARE = 4
N_STRIP = 4
N_DEPTH = 8


def draw_occupancy(key, part):
    level_key = jax.random.fold_in(key, 11)
    value_key = jax.random.fold_in(key, 12)
    levels = jax.random.randint(level_key, (N_DEPTH, 1, 1), 2, 9)
    values = jax.random.randint(value_key, (N_DEPTH, HEIGHT // BRICK_ROWS, WIDTH // BRICK_COLS), 0, 8)
    return (values < levels).astype(jnp.int32)


def draw_slab_order(key, part):
    indices = jnp.arange(N_DEPTH, dtype=jnp.int32)
    order_now = indices
    bit_total = N_DEPTH.bit_length() - 1
    for bit_index in range(bit_total):
        flips = jax.random.randint(jax.random.fold_in(key, 30 + bit_index), (N_DEPTH,), 0, 2).astype(jnp.int32)
        chosen = jnp.take(flips, jnp.right_shift(indices, bit_index + 1))
        order_now = jnp.bitwise_xor(order_now, jnp.left_shift(chosen, bit_index)).astype(jnp.int32)
    return order_now.astype(jnp.int32)


def steps_of(rng, dims, shards, low, high):
    gain = 1.0
    for dim, shards_of in shards:
        draws = jax.random.uniform(jax.random.fold_in(jax.random.fold_in(rng, 6), dim), (shards_of,), jnp.float32, low / len(shards), high / len(shards))
        gain = gain * jnp.repeat(jnp.exp(draws), dims[dim] // shards_of).reshape((-1,) + (1,) * (len(dims) - 1 - dim))
    return gain


def bell_draw(rng, dims, scale, bound, pieces=(), kind=jnp.bfloat16):
    entries = scale * jax.random.normal(rng, dims, jnp.float32)
    if pieces:
        entries = entries * steps_of(rng, dims, pieces, -0.22, 0.18)
    return jnp.clip(entries, -bound, bound).astype(kind)


def setup_inputs(seed: int = 0) -> dict:
    seeds = jax.random.split(jax.random.key(seed), 10)
    volume = bell_draw(seeds[0], (DEPTH, HEIGHT, WIDTH), 1.0, 6.0, ((0, 8), (1, 4)))
    occupancy = draw_occupancy(jax.random.fold_in(seeds[9], 71), 0)
    slab_order = draw_slab_order(jax.random.fold_in(seeds[9], 71), 0)
    w_in = bell_draw(seeds[3], (CHANNELS, HIDDEN_SIZE), CHANNELS ** -0.5, 3.0)
    b_in = bell_draw(seeds[4], (HIDDEN_SIZE,), 0.5, 3.0, (), jnp.float32)
    w_out = bell_draw(seeds[5], (HIDDEN_SIZE, CHANNELS), 0.25, 1.5)
    b_out = bell_draw(seeds[6], (CHANNELS,), 1.0, 3.0, (), jnp.float32)
    conv_weight = bell_draw(seeds[7], (3, 3, 3, 3), 27 ** -0.5, 1.25, (), jnp.float32)
    conv_bias = bell_draw(seeds[8], (3,), 0.5, 3.0, (), jnp.float32)
    return dict(volume=volume, occupancy=occupancy, slab_order=slab_order, w_in=w_in, b_in=b_in, w_out=w_out, b_out=b_out, conv_weight=conv_weight, conv_bias=conv_bias)


def expand_bricks(bricks):
    brick_rows_n, brick_cols_n = bricks.shape
    spread = jnp.broadcast_to(bricks.astype(jnp.float32)[:, None, :, None], (brick_rows_n, BRICK_ROWS, brick_cols_n, BRICK_COLS))
    return spread.reshape(brick_rows_n * BRICK_ROWS, brick_cols_n * BRICK_COLS)


def march_slab(features, coverage, w_in, b_in, w_out, b_out, optical):
    rows_all = features.shape[2]
    cols_all = features.shape[3]

    def layer_step(state_pair, layer_feats):
        colour_sum, remaining = state_pair
        flattened = layer_feats.reshape(4, rows_all * cols_all)
        hidden = jax.nn.silu(jnp.dot(w_in.T, flattened, preferred_element_type=jnp.float32) + b_in[:, None]).astype(jnp.bfloat16)
        output = jnp.dot(w_out.T, hidden, preferred_element_type=jnp.float32) + b_out[:, None]
        output = output.reshape(4, rows_all, cols_all)
        colour = jax.nn.sigmoid(output[:3])
        density = jax.nn.softplus(output[3]) * coverage
        alpha_val = 1.0 - jnp.exp(-optical * density)
        colour_sum = colour_sum + (remaining * alpha_val)[None] * colour
        remaining = remaining * (1.0 - alpha_val)
        return (colour_sum, remaining), None

    start = (jnp.zeros((3, rows_all, cols_all), jnp.float32), jnp.ones((rows_all, cols_all), jnp.float32))
    (colour_sum, remaining), unused = lax.scan(layer_step, start, features)
    return colour_sum, remaining


def slab_features(slab_field):
    scalar_field = slab_field.astype(jnp.float32)
    padded_cols = jnp.pad(scalar_field, ((0, 0), (0, 0), (1, 1)))
    grad_cols = 0.5 * (padded_cols[:, :, 2:] - padded_cols[:, :, :-2])
    padded_rows = jnp.pad(scalar_field, ((0, 0), (1, 1), (0, 0)))
    grad_rows = 0.5 * (padded_rows[:, 2:] - padded_rows[:, :-2])
    padded_depth = jnp.concatenate([scalar_field[:1], scalar_field, scalar_field[-1:]], 0)
    grad_depth = 0.5 * (padded_depth[2:] - padded_depth[:-2])
    return jnp.stack([scalar_field, grad_cols, grad_rows, grad_depth], 1).astype(jnp.bfloat16)


def denoise(picture, conv_weight, conv_bias):
    rows_all = picture.shape[1]
    cols_all = picture.shape[2]
    padded = jnp.pad(picture, ((0, 0), (1, 1), (1, 1)))
    filtered = jnp.broadcast_to(conv_bias[:, None, None], (3, rows_all, cols_all))
    for row_off in range(3):
        for col_off in range(3):
            window = padded[:, row_off:row_off + rows_all, col_off:col_off + cols_all]
            filtered = filtered + jnp.sum(conv_weight[:, :, row_off, col_off][:, :, None, None] * window[None], axis=1)
    return filtered


def reference(volume, occupancy, slab_order, w_in, b_in, w_out, b_out, conv_weight, conv_bias):
    optical = 2.0 / DEPTH
    inverse = jnp.argsort(slab_order).astype(jnp.int32)

    def composite(state_pair, position):
        colour_acc, remaining_acc = state_pair
        slab_index = inverse[position].astype(jnp.int32)
        slab_field = lax.dynamic_slice_in_dim(volume, (slab_index * Z_DEV).astype(jnp.int32), Z_DEV, 0)
        coverage = expand_bricks(lax.dynamic_index_in_dim(occupancy, slab_index, 0, keepdims=False))
        colour_slab, remaining_slab = march_slab(slab_features(slab_field), coverage, w_in, b_in, w_out, b_out, optical)
        return (colour_acc + remaining_acc[None] * colour_slab, remaining_acc * remaining_slab), None

    start = (jnp.zeros((3, HEIGHT, WIDTH), jnp.float32), jnp.ones((HEIGHT, WIDTH), jnp.float32))
    (picture, remaining_end), unused = lax.scan(composite, start, jnp.arange(N_DEPTH, dtype=jnp.int32))
    filtered = denoise(picture, conv_weight, conv_bias)
    return filtered.reshape(3, N_STRIP, ROW_SHARE, N_DEPTH, WIDTH)
```

```python
import functools

import jax
import jax.numpy as jnp
import numpy as np
from jax import lax
from jax.experimental import pallas as pl
from jax.experimental.pallas import tpu as pltpu
from jax.sharding import PartitionSpec as P

def with_halo(cells, sides, width, closed):
    for axis, dim in sides:
        count = lax.axis_size(axis)
        ends = count if closed else count - 1
        head = lax.slice_in_dim(cells, 0, width, axis=dim)
        tail = lax.slice_in_dim(cells, cells.shape[dim] - width, cells.shape[dim], axis=dim)
        cells = jnp.concatenate(
            [
                lax.ppermute(tail, axis, [(i, (i + 1) % count) for i in range(ends)]),
                cells,
                lax.ppermute(head, axis, [((i + 1) % count, i) for i in range(ends)]),
            ],
            axis=dim,
        )
    return cells


def partner(block, axis, stride):
    count = lax.axis_size(axis)
    route = []
    for low in range(count):
        high = low | 1 << stride
        if high != low and high < count:
            route += [(low, high), (high, low)]
    return lax.ppermute(block, axis, route)


LANES = 128


def march_kernel(optical, unroll, occ_ref, vol_ref, above_ref, below_ref, lhs_ref, mix_ref, bias_ref, out_ref, feat, picks):
    layers, rows, cols = vol_ref.shape
    bricks = occ_ref.shape[0]
    tiles = out_ref.shape[0]
    lane = lax.broadcasted_iota(jnp.int32, (rows, cols), 1)
    row = lax.broadcasted_iota(jnp.int32, (rows, cols), 0)
    first_col, last_col = lane == 0, lane == cols - 1
    first_row, last_row = row == 0, row == rows - 1
    ones = jnp.ones((feat.shape[1] - 4 * rows, cols), jnp.bfloat16)

    def features(z, carry):
        here = vol_ref[z].astype(jnp.float32)
        right = jnp.where(last_col, 0.0, pltpu.roll(here, cols - 1, 1))
        left = jnp.where(first_col, 0.0, pltpu.roll(here, 1, 1))
        down = jnp.where(last_row, below_ref[z].astype(jnp.float32), pltpu.roll(here, rows - 1, 0))
        up = jnp.where(first_row, above_ref[z].astype(jnp.float32), pltpu.roll(here, 1, 0))
        far = vol_ref[jnp.minimum(z + 1, layers - 1)].astype(jnp.float32)
        near = vol_ref[jnp.maximum(z - 1, 0)].astype(jnp.float32)
        feat[z, 0:rows] = vol_ref[z]
        feat[z, rows:2 * rows] = (0.5 * (right - left)).astype(jnp.bfloat16)
        feat[z, 2 * rows:3 * rows] = (0.5 * (down - up)).astype(jnp.bfloat16)
        feat[z, 3 * rows:4 * rows] = (0.5 * (far - near)).astype(jnp.bfloat16)
        feat[z, 4 * rows:] = ones
        return carry

    lax.fori_loop(0, layers, features, 0)
    out_ref[:, :3] = jnp.zeros((tiles, 3, 8, cols), jnp.float32)
    out_ref[:, 3:] = jnp.ones((tiles, 1, 8, cols), jnp.float32)

    def pick(i, found):
        picks[found] = i
        return found + (occ_ref[i] != 0).astype(jnp.int32)

    found = lax.fori_loop(0, bricks, pick, 0)

    def pair(step, carry):
        part = step // tiles
        tile = step % tiles
        low = pl.ds(pl.multiple_of(picks[2 * part] * LANES, LANES), LANES)
        high = pl.ds(pl.multiple_of(picks[jnp.minimum(2 * part + 1, found - 1)] * LANES, LANES), LANES)

        def layer(z, state):
            colour, remaining = state
            x = jnp.concatenate([feat[z, :, low], feat[z, :, high]], 1)
            out = bias_ref[...]
            for p in range(2):
                u = jnp.dot(lhs_ref[2 * tile + p], x, preferred_element_type=jnp.float32)
                hidden = (u + u * jnp.tanh(u)).astype(jnp.bfloat16)
                out = out + jnp.dot(mix_ref[p], hidden, preferred_element_type=jnp.float32)
            raw = out[24:32]
            density = jnp.maximum(raw, 0.0) + jnp.log1p(jnp.exp(-jnp.abs(raw)))
            keep = jnp.exp(-optical * density)
            weight = 0.5 * (remaining * (1.0 - keep))
            colour = tuple(
                colour[i] + (weight + weight * jnp.tanh(out[8 * i:8 * i + 8])) for i in range(3)
            )
            return colour, remaining * keep

        zero = jnp.zeros((8, 2 * LANES), jnp.float32)
        state = ((zero, zero, zero), jnp.ones((8, 2 * LANES), jnp.float32))

        def layer_group(group, state):
            for k in range(unroll):
                state = layer(group * unroll + k, state)
            return state

        if unroll == layers:
            state = layer_group(0, state)
        else:
            state = lax.fori_loop(0, layers // unroll, layer_group, state)
        colour, remaining = state
        for i, value in enumerate(colour + (remaining,)):
            out_ref[tile, i, :, low] = value[:, :LANES]
            out_ref[tile, i, :, high] = value[:, LANES:]
        return carry

    lax.fori_loop(0, (found + 1) // 2 * tiles, pair, 0)


def march(volume, above, below, occupancy, w_in, b_in, w_out, b_out, depth_count, optical):
    layers, rows, cols = volume.shape
    channels, hidden = w_in.shape
    tiles = rows // 8
    share = rows // depth_count
    pos_row = np.zeros((tiles, 8), np.int64)
    for r in range(rows):
        d, k = r % depth_count, r // depth_count
        pos_row[d % tiles, d // tiles * share + k] = r
    chosen = np.zeros((rows, rows), np.float32)
    chosen[np.arange(rows), pos_row.reshape(-1)] = 1.0
    half_in = 0.5 * w_in.astype(jnp.float32)
    spread = jnp.asarray(chosen)[:, None, None, :] * half_in.T[None, :, :, None]
    spread = spread.reshape(rows * hidden, channels * rows)
    rest = 0.5 * b_in
    parts = []
    for unused in range(3):
        part = lax.reduce_precision(rest, 8, 7)
        parts.append(part)
        rest = rest - part
    parts = jnp.stack(parts + [jnp.zeros_like(b_in)] * 13, 1)
    parts = jnp.broadcast_to(parts[None], (rows, hidden, 16)).reshape(rows * hidden, 16)
    lhs = jnp.concatenate([spread, parts], 1).astype(jnp.bfloat16)
    lhs = lhs.reshape(2 * tiles, 4 * hidden, channels * rows + 16)
    scale = jnp.asarray(np.array([0.5, 0.5, 0.5, 1.0], np.float32))
    place = np.zeros((2, 8, 4), np.float32)
    for p in range(2):
        for i in range(4):
            place[p, 4 * p + i, i] = 1.0
    scaled_out = w_out.astype(jnp.float32) * scale[None]
    mix = scaled_out.T[None, :, None, None, :] * jnp.asarray(place)[:, None, :, :, None]
    mix = mix.reshape(2, 32, 4 * hidden).astype(jnp.bfloat16)
    bias = jnp.broadcast_to((b_out * scale)[:, None, None], (4, 8, 2 * LANES)).reshape(32, 2 * LANES)
    vmem = pl.BlockSpec(memory_space=pltpu.VMEM)
    return pl.pallas_call(
        functools.partial(march_kernel, optical, 8),
        out_shape=jax.ShapeDtypeStruct((tiles, 4, 8, cols), jnp.float32),
        in_specs=[pl.BlockSpec(memory_space=pltpu.SMEM)] + [vmem] * 6,
        out_specs=vmem,
        scratch_shapes=[
            pltpu.VMEM((layers, channels * rows + 16, cols), jnp.bfloat16),
            pltpu.SMEM((occupancy.size + 1,), jnp.int32),
        ],
        compiler_params=pltpu.CompilerParams(vmem_limit_bytes=40 * 1024 * 1024),
        name="march",
    )(occupancy.reshape(-1), volume, above, below, lhs, mix, bias)


def over_pair(front_part, back_part):
    colour = front_part[:3] + front_part[3:4] * back_part[:3]
    remaining = front_part[3:4] * back_part[3:4]
    return jnp.concatenate([colour, remaining], 0)


def shards(volume, occupancy, slab_order, w_in, b_in, w_out, b_out, conv_weight, conv_bias):
    depth_count = lax.axis_size("depth")
    depth_index = lax.axis_index("depth")
    strip_count = lax.axis_size("strip")
    strip_index = lax.axis_index("strip")
    layers, rows_here, columns = volume.shape
    optical = 2.0 / (layers * depth_count)
    down_route = [(i, i + 1) for i in range(strip_count - 1)]
    up_route = [(i + 1, i) for i in range(strip_count - 1)]
    above = lax.ppermute(volume[:, rows_here - 1 :], "strip", down_route)
    below = lax.ppermute(volume[:, :1], "strip", up_route)
    partial_value = march(
        volume, above, below, occupancy, w_in, b_in, w_out, b_out, depth_count, optical
    )
    own_order = slab_order[depth_index]
    rounds = depth_count.bit_length() - 1
    row_share = rows_here // depth_count
    tiles = partial_value.shape[0]
    composed = partial_value.transpose(1, 0, 2, 3)
    for bit_index in range(rounds):
        if composed.shape[1] > 1:
            paired = composed.reshape(4, composed.shape[1] // 2, 2, composed.shape[2], columns)
        else:
            paired = composed.reshape(4, composed.shape[2] // 2 // row_share, 2, row_share, columns)
        mine_bit = jnp.bitwise_and(jnp.right_shift(depth_index, bit_index), 1)
        keep_part = jnp.where(mine_bit == 0, paired[:, :, 0], paired[:, :, 1])
        give_part = jnp.where(mine_bit == 0, paired[:, :, 1], paired[:, :, 0])
        received = partner(give_part, "depth", bit_index)
        in_front = jnp.bitwise_and(jnp.right_shift(own_order, bit_index), 1) == 0
        front_part = jnp.where(in_front, keep_part, received)
        back_part = jnp.where(in_front, received, keep_part)
        composed = over_pair(front_part, back_part)
        if paired.shape[3] == row_share and tiles >> (bit_index + 1) < 1:
            composed = composed.reshape(4, 1, -1, columns)
    composed = composed.reshape(4, row_share, columns)
    picture = composed[:3][:, :, None, :]
    extended = with_halo(picture, (("strip", 1), ("depth", 2)), 1, True)
    edge_weight = jnp.concatenate(
        [
            (strip_index > 0).astype(jnp.float32)[None],
            jnp.ones((row_share,), jnp.float32),
            (strip_index < strip_count - 1).astype(jnp.float32)[None],
        ],
        0,
    )
    extended = extended * edge_weight[None, :, None, None]
    row_centre = extended[:, 1 : row_share + 1, 1]
    row_above = jnp.where(
        depth_index == 0, extended[:, 0:row_share, 0], extended[:, 1 : row_share + 1, 0]
    )
    row_below = jnp.where(
        depth_index == depth_count - 1,
        extended[:, 2 : row_share + 2, 2],
        extended[:, 1 : row_share + 1, 2],
    )
    row_sets = [row_above, row_centre, row_below]
    filtered = jnp.broadcast_to(conv_bias[:, None, None], (3, row_share, columns))
    for row_off in range(3):
        padded = jnp.pad(row_sets[row_off], ((0, 0), (0, 0), (1, 1)))
        for col_off in range(3):
            window = padded[:, :, col_off : col_off + columns]
            filtered = filtered + jnp.sum(
                conv_weight[:, :, row_off, col_off][:, :, None, None] * window[None], axis=1
            )
    return filtered.reshape(3, 1, row_share, 1, columns)


def solution(mesh):
    placed = (
        P("depth", "strip", None),
        P("depth", "strip", None),
        P(),
        P(),
        P(),
        P(),
        P(),
        P(),
        P(),
    )
    return jax.shard_map(
        shards,
        mesh=mesh,
        in_specs=placed,
        out_specs=P(None, "strip", None, "depth", None),
        check_vma=False,
    )
```

```python
import functools

import jax
import jax.numpy as jnp
import numpy as np
from jax import lax
from jax.experimental import pallas as pl
from jax.experimental.pallas import tpu as pltpu
from jax.sharding import PartitionSpec as P

def partner(block, axis, stride):
    count = lax.axis_size(axis)
    route = []
    for low in range(count):
        high = low | 1 << stride
        if high != low and high < count:
            route += [(low, high), (high, low)]
    return lax.ppermute(block, axis, route)


LANES = 128


def march_kernel(optical, unroll, group, occ_ref, vol_ref, above_ref, below_ref, lhs_ref, mix_ref, bias_ref, out_ref, feat, picks):
    layers, rows, cols = vol_ref.shape
    bricks = occ_ref.shape[0]
    tiles = out_ref.shape[0]
    lane = lax.broadcasted_iota(jnp.int32, (rows, cols), 1)
    row = lax.broadcasted_iota(jnp.int32, (rows, cols), 0)
    first_col, last_col = lane == 0, lane == cols - 1
    first_row, last_row = row == 0, row == rows - 1
    ones = jnp.ones((feat.shape[1] - 4 * rows, cols), jnp.bfloat16)

    def features(z, carry):
        here = vol_ref[z].astype(jnp.float32)
        right = jnp.where(last_col, 0.0, pltpu.roll(here, cols - 1, 1))
        left = jnp.where(first_col, 0.0, pltpu.roll(here, 1, 1))
        down = jnp.where(last_row, below_ref[z].astype(jnp.float32), pltpu.roll(here, rows - 1, 0))
        up = jnp.where(first_row, above_ref[z].astype(jnp.float32), pltpu.roll(here, 1, 0))
        far = vol_ref[jnp.minimum(z + 1, layers - 1)].astype(jnp.float32)
        near = vol_ref[jnp.maximum(z - 1, 0)].astype(jnp.float32)
        feat[z, 0:rows] = vol_ref[z]
        feat[z, rows:2 * rows] = (0.5 * (right - left)).astype(jnp.bfloat16)
        feat[z, 2 * rows:3 * rows] = (0.5 * (down - up)).astype(jnp.bfloat16)
        feat[z, 3 * rows:4 * rows] = (0.5 * (far - near)).astype(jnp.bfloat16)
        feat[z, 4 * rows:] = ones
        return carry

    lax.fori_loop(0, layers, features, 0)
    out_ref[:, :3] = jnp.zeros((tiles, 3, 8, cols), jnp.float32)
    out_ref[:, 3:] = jnp.ones((tiles, 1, 8, cols), jnp.float32)

    def pick(i, found):
        picks[found] = i
        return found + (occ_ref[i] != 0).astype(jnp.int32)

    found = lax.fori_loop(0, bricks, pick, 0)

    def pair(step, carry):
        part = step // (tiles // group)
        first_tile = step % (tiles // group) * group
        low = pl.ds(pl.multiple_of(picks[2 * part] * LANES, LANES), LANES)
        high = pl.ds(pl.multiple_of(picks[jnp.minimum(2 * part + 1, found - 1)] * LANES, LANES), LANES)

        def layer(z, states):
            x = jnp.concatenate([feat[z, :, low], feat[z, :, high]], 1)
            lhs = lhs_ref[pl.ds(first_tile, group)].reshape(-1, lhs_ref.shape[2])
            us = jnp.dot(lhs, x, preferred_element_type=jnp.float32)
            fresh = []
            span = us.shape[0] // group // 2
            for t, (colour, remaining) in enumerate(states):
                out = bias_ref[...]
                for p in range(2):
                    at = (2 * t + p) * span
                    u = us[at:at + span]
                    hidden = (u + u * jnp.tanh(u)).astype(jnp.bfloat16)
                    out = out + jnp.dot(mix_ref[p], hidden, preferred_element_type=jnp.float32)
                raw = out[24:32]
                density = jnp.maximum(raw, 0.0) + jnp.log1p(jnp.exp(-jnp.abs(raw)))
                keep = jnp.exp(-optical * density)
                weight = 0.5 * (remaining * (1.0 - keep))
                colour = tuple(
                    colour[i] + (weight + weight * jnp.tanh(out[8 * i:8 * i + 8])) for i in range(3)
                )
                fresh.append((colour, remaining * keep))
            return tuple(fresh)

        zero = jnp.zeros((8, 2 * LANES), jnp.float32)
        states = (((zero, zero, zero), jnp.ones((8, 2 * LANES), jnp.float32)),) * group

        def layer_group(step_z, states):
            for k in range(unroll):
                states = layer(step_z * unroll + k, states)
            return states

        if unroll == layers:
            states = layer_group(0, states)
        else:
            states = lax.fori_loop(0, layers // unroll, layer_group, states)
        for t, (colour, remaining) in enumerate(states):
            for i, value in enumerate(colour + (remaining,)):
                out_ref[first_tile + t, i, :, low] = value[:, :LANES]
                out_ref[first_tile + t, i, :, high] = value[:, LANES:]
        return carry

    lax.fori_loop(0, (found + 1) // 2 * (tiles // group), pair, 0)


def march(volume, above, below, occupancy, w_in, b_in, w_out, b_out, depth_count, optical):
    layers, rows, cols = volume.shape
    channels, hidden = w_in.shape
    tiles = rows // 8
    share = rows // depth_count
    pos_row = np.zeros((tiles, 8), np.int64)
    for r in range(rows):
        d, k = r % depth_count, r // depth_count
        pos_row[d % tiles, d // tiles * share + k] = r
    chosen = np.zeros((rows, rows), np.float32)
    chosen[np.arange(rows), pos_row.reshape(-1)] = 1.0
    half_in = 0.5 * w_in.astype(jnp.float32)
    spread = jnp.asarray(chosen)[:, None, None, :] * half_in.T[None, :, :, None]
    spread = spread.reshape(rows * hidden, channels * rows)
    rest = 0.5 * b_in
    parts = []
    for unused in range(3):
        part = lax.reduce_precision(rest, 8, 7)
        parts.append(part)
        rest = rest - part
    parts = jnp.stack(parts + [jnp.zeros_like(b_in)] * 13, 1)
    parts = jnp.broadcast_to(parts[None], (rows, hidden, 16)).reshape(rows * hidden, 16)
    lhs = jnp.concatenate([spread, parts], 1).astype(jnp.bfloat16)
    lhs = lhs.reshape(tiles, 8 * hidden, channels * rows + 16)
    scale = jnp.asarray(np.array([0.5, 0.5, 0.5, 1.0], np.float32))
    place = np.zeros((2, 8, 4), np.float32)
    for p in range(2):
        for i in range(4):
            place[p, 4 * p + i, i] = 1.0
    scaled_out = w_out.astype(jnp.float32) * scale[None]
    mix = scaled_out.T[None, :, None, None, :] * jnp.asarray(place)[:, None, :, :, None]
    mix = mix.reshape(2, 32, 4 * hidden).astype(jnp.bfloat16)
    bias = jnp.broadcast_to((b_out * scale)[:, None, None], (4, 8, 2 * LANES)).reshape(32, 2 * LANES)
    vmem = pl.BlockSpec(memory_space=pltpu.VMEM)
    return pl.pallas_call(
        functools.partial(march_kernel, optical, layers, tiles),
        out_shape=jax.ShapeDtypeStruct((tiles, 4, 8, cols), jnp.float32),
        in_specs=[pl.BlockSpec(memory_space=pltpu.SMEM)] + [vmem] * 6,
        out_specs=vmem,
        scratch_shapes=[
            pltpu.VMEM((layers, channels * rows + 16, cols), jnp.bfloat16),
            pltpu.SMEM((occupancy.size + 1,), jnp.int32),
        ],
        compiler_params=pltpu.CompilerParams(vmem_limit_bytes=40 * 1024 * 1024),
        name="march",
    )(occupancy.reshape(-1), volume, above, below, lhs, mix, bias)


def over_pair(front_part, back_part):
    colour = front_part[:3] + front_part[3:4] * back_part[:3]
    remaining = front_part[3:4] * back_part[3:4]
    return jnp.concatenate([colour, remaining], 0)


def shards(volume, occupancy, slab_order, w_in, b_in, w_out, b_out, conv_weight, conv_bias):
    depth_count = lax.axis_size("depth")
    depth_index = lax.axis_index("depth")
    strip_count = lax.axis_size("strip")
    layers, rows_here, columns = volume.shape
    optical = 2.0 / (layers * depth_count)
    down_route = [(i, i + 1) for i in range(strip_count - 1)]
    up_route = [(i + 1, i) for i in range(strip_count - 1)]
    above = lax.ppermute(volume[:, rows_here - 1 :], "strip", down_route)
    below = lax.ppermute(volume[:, :1], "strip", up_route)
    partial_value = march(
        volume, above, below, occupancy, w_in, b_in, w_out, b_out, depth_count, optical
    )
    own_order = slab_order[depth_index]
    rounds = depth_count.bit_length() - 1
    row_share = rows_here // depth_count
    tiles = partial_value.shape[0]
    composed = partial_value.transpose(1, 0, 2, 3)
    for bit_index in range(rounds):
        if composed.shape[1] > 1:
            paired = composed.reshape(4, composed.shape[1] // 2, 2, composed.shape[2], columns)
        else:
            paired = composed.reshape(4, composed.shape[2] // 2 // row_share, 2, row_share, columns)
        mine_bit = jnp.bitwise_and(jnp.right_shift(depth_index, bit_index), 1)
        keep_part = jnp.where(mine_bit == 0, paired[:, :, 0], paired[:, :, 1])
        give_part = jnp.where(mine_bit == 0, paired[:, :, 1], paired[:, :, 0])
        received = partner(give_part, "depth", bit_index)
        in_front = jnp.bitwise_and(jnp.right_shift(own_order, bit_index), 1) == 0
        front_part = jnp.where(in_front, keep_part, received)
        back_part = jnp.where(in_front, received, keep_part)
        composed = over_pair(front_part, back_part)
        if paired.shape[3] == row_share and tiles >> (bit_index + 1) < 1:
            composed = composed.reshape(4, 1, -1, columns)
    composed = composed.reshape(4, row_share, columns)
    picture = composed[:3]
    ring = [(i, (i + 1) % depth_count) for i in range(depth_count)]
    back = [(j, i) for i, j in ring]
    last = depth_count - 1
    corner = [(i * depth_count + last, (i + 1) * depth_count) for i in range(strip_count - 1)]
    corner_back = [(j, i) for i, j in corner]
    from_above = lax.ppermute(picture, "depth", ring)
    from_below = lax.ppermute(picture, "depth", back)
    strip_above = lax.ppermute(picture[:, row_share - 1 :], ("strip", "depth"), corner)
    strip_below = lax.ppermute(picture[:, :1], ("strip", "depth"), corner_back)
    row_above = jnp.where(
        depth_index == 0,
        jnp.concatenate([strip_above, from_above[:, : row_share - 1]], 1),
        from_above,
    )
    row_below = jnp.where(
        depth_index == last,
        jnp.concatenate([from_below[:, 1:], strip_below], 1),
        from_below,
    )
    row_centre = picture
    row_sets = [row_above, row_centre, row_below]
    filtered = jnp.broadcast_to(conv_bias[:, None, None], (3, row_share, columns))
    for row_off in range(3):
        padded = jnp.pad(row_sets[row_off], ((0, 0), (0, 0), (1, 1)))
        for col_off in range(3):
            window = padded[:, :, col_off : col_off + columns]
            filtered = filtered + jnp.sum(
                conv_weight[:, :, row_off, col_off][:, :, None, None] * window[None], axis=1
            )
    return filtered.reshape(3, 1, row_share, 1, columns)


def solution(mesh):
    placed = (
        P("depth", "strip", None),
        P("depth", "strip", None),
        P(),
        P(),
        P(),
        P(),
        P(),
        P(),
        P(),
    )
    return jax.shard_map(
        shards,
        mesh=mesh,
        in_specs=placed,
        out_specs=P(None, "strip", None, "depth", None),
        check_vma=False,
    )
```

```python
import functools

import jax
import jax.numpy as jnp
import numpy as np
from jax import lax
from jax.experimental import pallas as pl
from jax.experimental.pallas import tpu as pltpu
from jax.sharding import PartitionSpec as P

def partner(block, axis, stride):
    count = lax.axis_size(axis)
    route = []
    for low in range(count):
        high = low | 1 << stride
        if high != low and high < count:
            route += [(low, high), (high, low)]
    return lax.ppermute(block, axis, route)


LANES = 128


def march_kernel(optical, unroll, group, depth_count, occ_ref, vol_ref, above_ref, below_ref, pattern_ref, mix_ref, bias_ref, out_ref, feat, lhs_ref, picks):
    layers, rows, cols = vol_ref.shape
    bricks = occ_ref.shape[0]
    tiles = out_ref.shape[0]
    lane = lax.broadcasted_iota(jnp.int32, (rows, cols), 1)
    row = lax.broadcasted_iota(jnp.int32, (rows, cols), 0)
    first_col, last_col = lane == 0, lane == cols - 1
    first_row, last_row = row == 0, row == rows - 1
    ones = jnp.ones((feat.shape[1] - 4 * rows, cols), jnp.bfloat16)

    def features(z, carry):
        here = vol_ref[z].astype(jnp.float32)
        right = jnp.where(last_col, 0.0, pltpu.roll(here, cols - 1, 1))
        left = jnp.where(first_col, 0.0, pltpu.roll(here, 1, 1))
        down = jnp.where(last_row, below_ref[z].astype(jnp.float32), pltpu.roll(here, rows - 1, 0))
        up = jnp.where(first_row, above_ref[z].astype(jnp.float32), pltpu.roll(here, 1, 0))
        far = vol_ref[jnp.minimum(z + 1, layers - 1)].astype(jnp.float32)
        near = vol_ref[jnp.maximum(z - 1, 0)].astype(jnp.float32)
        feat[z, 0:rows] = vol_ref[z]
        feat[z, rows:2 * rows] = (0.5 * (right - left)).astype(jnp.bfloat16)
        feat[z, 2 * rows:3 * rows] = (0.5 * (down - up)).astype(jnp.bfloat16)
        feat[z, 3 * rows:4 * rows] = (0.5 * (far - near)).astype(jnp.bfloat16)
        feat[z, 4 * rows:] = ones
        return carry

    lax.fori_loop(0, layers, features, 0)
    pattern = pattern_ref[...]
    hidden_size = pattern.shape[0]
    source = lax.broadcasted_iota(jnp.int32, pattern.shape, 1)
    source = jnp.where(source < 4 * rows, source % rows, -1)
    share = rows // depth_count
    for r in range(rows):
        d, k = r % depth_count, r // depth_count
        at = (d // tiles * share + k) * hidden_size
        entry = jnp.where((source == r) | (source < 0), pattern, 0.0)
        lhs_ref[d % tiles, at:at + hidden_size] = entry.astype(jnp.bfloat16)
    out_ref[:, :3] = jnp.zeros((tiles, 3, 8, cols), jnp.float32)
    out_ref[:, 3:] = jnp.ones((tiles, 1, 8, cols), jnp.float32)

    def pick(i, found):
        picks[found] = i
        return found + (occ_ref[i] != 0).astype(jnp.int32)

    found = lax.fori_loop(0, bricks, pick, 0)

    def pair(step, carry):
        part = step // (tiles // group)
        first_tile = step % (tiles // group) * group
        low = pl.ds(pl.multiple_of(picks[2 * part] * LANES, LANES), LANES)
        high = pl.ds(pl.multiple_of(picks[jnp.minimum(2 * part + 1, found - 1)] * LANES, LANES), LANES)

        def layer(z, states):
            x = jnp.concatenate([feat[z, :, low], feat[z, :, high]], 1)
            lhs = lhs_ref[pl.ds(first_tile, group)].reshape(-1, lhs_ref.shape[2])
            us = jnp.dot(lhs, x, preferred_element_type=jnp.float32)
            fresh = []
            span = us.shape[0] // group // 2
            for t, (colour, remaining) in enumerate(states):
                out = bias_ref[...]
                for p in range(2):
                    at = (2 * t + p) * span
                    u = us[at:at + span]
                    hidden = (u + u * jnp.tanh(u)).astype(jnp.bfloat16)
                    out = out + jnp.dot(mix_ref[p], hidden, preferred_element_type=jnp.float32)
                raw = out[24:32]
                density = jnp.maximum(raw, 0.0) + jnp.log1p(jnp.exp(-jnp.abs(raw)))
                keep = jnp.exp(-optical * density)
                weight = 0.5 * (remaining * (1.0 - keep))
                colour = tuple(
                    colour[i] + (weight + weight * jnp.tanh(out[8 * i:8 * i + 8])) for i in range(3)
                )
                fresh.append((colour, remaining * keep))
            return tuple(fresh)

        zero = jnp.zeros((8, 2 * LANES), jnp.float32)
        states = (((zero, zero, zero), jnp.ones((8, 2 * LANES), jnp.float32)),) * group

        def layer_group(step_z, states):
            for k in range(unroll):
                states = layer(step_z * unroll + k, states)
            return states

        if unroll == layers:
            states = layer_group(0, states)
        else:
            states = lax.fori_loop(0, layers // unroll, layer_group, states)
        for t, (colour, remaining) in enumerate(states):
            for i, value in enumerate(colour + (remaining,)):
                out_ref[first_tile + t, i, :, low] = value[:, :LANES]
                out_ref[first_tile + t, i, :, high] = value[:, LANES:]
        return carry

    lax.fori_loop(0, (found + 1) // 2 * (tiles // group), pair, 0)


def march(volume, above, below, occupancy, w_in, b_in, w_out, b_out, depth_count, optical):
    layers, rows, cols = volume.shape
    channels, hidden = w_in.shape
    tiles = rows // 8
    share = rows // depth_count
    half_in = 0.5 * w_in.astype(jnp.float32)
    rest = 0.5 * b_in
    parts = []
    for unused in range(3):
        part = lax.reduce_precision(rest, 8, 7)
        parts.append(part)
        rest = rest - part
    wide = jnp.repeat(half_in.T, rows, axis=1)
    bias_in = jnp.pad(jnp.stack(parts, 1), ((0, 0), (0, 13)))
    pattern = jnp.concatenate([wide, bias_in], 1)
    scale = jnp.asarray(np.array([0.5, 0.5, 0.5, 1.0], np.float32))
    place = np.zeros((2, 8, 4), np.float32)
    for p in range(2):
        for i in range(4):
            place[p, 4 * p + i, i] = 1.0
    scaled_out = w_out.astype(jnp.float32) * scale[None]
    mix = scaled_out.T[None, :, None, None, :] * jnp.asarray(place)[:, None, :, :, None]
    mix = mix.reshape(2, 32, 4 * hidden).astype(jnp.bfloat16)
    bias = jnp.broadcast_to((b_out * scale)[:, None, None], (4, 8, 2 * LANES)).reshape(32, 2 * LANES)
    vmem = pl.BlockSpec(memory_space=pltpu.VMEM)
    return pl.pallas_call(
        functools.partial(march_kernel, optical, layers, tiles, depth_count),
        out_shape=jax.ShapeDtypeStruct((tiles, 4, 8, cols), jnp.float32),
        in_specs=[pl.BlockSpec(memory_space=pltpu.SMEM)] + [vmem] * 6,
        out_specs=vmem,
        scratch_shapes=[
            pltpu.VMEM((layers, channels * rows + 16, cols), jnp.bfloat16),
            pltpu.VMEM((tiles, 8 * hidden, channels * rows + 16), jnp.bfloat16),
            pltpu.SMEM((occupancy.size + 1,), jnp.int32),
        ],
        compiler_params=pltpu.CompilerParams(vmem_limit_bytes=40 * 1024 * 1024),
        name="march",
    )(occupancy.reshape(-1), volume, above, below, pattern, mix, bias)


def over_pair(front_part, back_part):
    colour = front_part[:3] + front_part[3:4] * back_part[:3]
    remaining = front_part[3:4] * back_part[3:4]
    return jnp.concatenate([colour, remaining], 0)


def shards(volume, occupancy, slab_order, w_in, b_in, w_out, b_out, conv_weight, conv_bias):
    depth_count = lax.axis_size("depth")
    depth_index = lax.axis_index("depth")
    strip_count = lax.axis_size("strip")
    layers, rows_here, columns = volume.shape
    optical = 2.0 / (layers * depth_count)
    down_route = [(i, i + 1) for i in range(strip_count - 1)]
    up_route = [(i + 1, i) for i in range(strip_count - 1)]
    above = lax.ppermute(volume[:, rows_here - 1 :], "strip", down_route)
    below = lax.ppermute(volume[:, :1], "strip", up_route)
    partial_value = march(
        volume, above, below, occupancy, w_in, b_in, w_out, b_out, depth_count, optical
    )
    own_order = slab_order[depth_index]
    rounds = depth_count.bit_length() - 1
    row_share = rows_here // depth_count
    tiles = partial_value.shape[0]
    composed = partial_value.transpose(1, 0, 2, 3)
    for bit_index in range(rounds):
        if composed.shape[1] > 1:
            paired = composed.reshape(4, composed.shape[1] // 2, 2, composed.shape[2], columns)
        else:
            paired = composed.reshape(4, composed.shape[2] // 2 // row_share, 2, row_share, columns)
        mine_bit = jnp.bitwise_and(jnp.right_shift(depth_index, bit_index), 1)
        keep_part = jnp.where(mine_bit == 0, paired[:, :, 0], paired[:, :, 1])
        give_part = jnp.where(mine_bit == 0, paired[:, :, 1], paired[:, :, 0])
        received = partner(give_part, "depth", bit_index)
        in_front = jnp.bitwise_and(jnp.right_shift(own_order, bit_index), 1) == 0
        front_part = jnp.where(in_front, keep_part, received)
        back_part = jnp.where(in_front, received, keep_part)
        composed = over_pair(front_part, back_part)
        if paired.shape[3] == row_share and tiles >> (bit_index + 1) < 1:
            composed = composed.reshape(4, 1, -1, columns)
    composed = composed.reshape(4, row_share, columns)
    picture = composed[:3]
    ring = [(i, (i + 1) % depth_count) for i in range(depth_count)]
    back = [(j, i) for i, j in ring]
    last = depth_count - 1
    corner = [(i * depth_count + last, (i + 1) * depth_count) for i in range(strip_count - 1)]
    corner_back = [(j, i) for i, j in corner]
    from_above = lax.ppermute(picture, "depth", ring)
    from_below = lax.ppermute(picture, "depth", back)
    strip_above = lax.ppermute(picture[:, row_share - 1 :], ("strip", "depth"), corner)
    strip_below = lax.ppermute(picture[:, :1], ("strip", "depth"), corner_back)
    row_above = jnp.where(
        depth_index == 0,
        jnp.concatenate([strip_above, from_above[:, : row_share - 1]], 1),
        from_above,
    )
    row_below = jnp.where(
        depth_index == last,
        jnp.concatenate([from_below[:, 1:], strip_below], 1),
        from_below,
    )
    row_centre = picture
    row_sets = [row_above, row_centre, row_below]
    filtered = jnp.broadcast_to(conv_bias[:, None, None], (3, row_share, columns))
    for row_off in range(3):
        padded = jnp.pad(row_sets[row_off], ((0, 0), (0, 0), (1, 1)))
        for col_off in range(3):
            window = padded[:, :, col_off : col_off + columns]
            filtered = filtered + jnp.sum(
                conv_weight[:, :, row_off, col_off][:, :, None, None] * window[None], axis=1
            )
    return filtered.reshape(3, 1, row_share, 1, columns)


def solution(mesh):
    placed = (
        P("depth", "strip", None),
        P("depth", "strip", None),
        P(),
        P(),
        P(),
        P(),
        P(),
        P(),
        P(),
    )
    return jax.shard_map(
        shards,
        mesh=mesh,
        in_specs=placed,
        out_specs=P(None, "strip", None, "depth", None),
        check_vma=False,
    )
```

```python
import functools

import jax
import jax.numpy as jnp
import numpy as np
from jax import lax
from jax.experimental import pallas as pl
from jax.experimental.pallas import tpu as pltpu
from jax.sharding import PartitionSpec as P

def partner(block, axis, stride):
    count = lax.axis_size(axis)
    route = []
    for low in range(count):
        high = low | 1 << stride
        if high != low and high < count:
            route += [(low, high), (high, low)]
    return lax.ppermute(block, axis, route)


LANES = 128


def march_kernel(optical, unroll, group, depth_count, occ_ref, vol_ref, above_ref, below_ref, pattern_ref, mix_ref, bias_ref, out_ref, feat, lhs_ref, picks):
    layers, rows, cols = vol_ref.shape
    bricks = occ_ref.shape[0]
    tiles = out_ref.shape[0]
    lane = lax.broadcasted_iota(jnp.int32, (rows, cols), 1)
    row = lax.broadcasted_iota(jnp.int32, (rows, cols), 0)
    first_col, last_col = lane == 0, lane == cols - 1
    first_row, last_row = row == 0, row == rows - 1
    ones = jnp.ones((feat.shape[1] - 4 * rows, cols), jnp.bfloat16)

    def features(z, carry):
        here = vol_ref[z].astype(jnp.float32)
        right = jnp.where(last_col, 0.0, pltpu.roll(here, cols - 1, 1))
        left = jnp.where(first_col, 0.0, pltpu.roll(here, 1, 1))
        down = jnp.where(last_row, below_ref[z].astype(jnp.float32), pltpu.roll(here, rows - 1, 0))
        up = jnp.where(first_row, above_ref[z].astype(jnp.float32), pltpu.roll(here, 1, 0))
        far = vol_ref[jnp.minimum(z + 1, layers - 1)].astype(jnp.float32)
        near = vol_ref[jnp.maximum(z - 1, 0)].astype(jnp.float32)
        feat[z, 0:rows] = vol_ref[z]
        feat[z, rows:2 * rows] = (0.5 * (right - left)).astype(jnp.bfloat16)
        feat[z, 2 * rows:3 * rows] = (0.5 * (down - up)).astype(jnp.bfloat16)
        feat[z, 3 * rows:4 * rows] = (0.5 * (far - near)).astype(jnp.bfloat16)
        feat[z, 4 * rows:] = ones
        return carry

    lax.fori_loop(0, layers, features, 0)
    pattern = pattern_ref[...]
    hidden_size = pattern.shape[0]
    source = lax.broadcasted_iota(jnp.int32, pattern.shape, 1)
    source = jnp.where(source < 4 * rows, source % rows, -1)
    share = rows // depth_count
    for r in range(rows):
        d, k = r % depth_count, r // depth_count
        at = (d // tiles * share + k) * hidden_size
        entry = jnp.where((source == r) | (source < 0), pattern, 0.0)
        lhs_ref[d % tiles, at:at + hidden_size] = entry.astype(jnp.bfloat16)
    out_ref[:, :3] = jnp.zeros((tiles, 3, 8, cols), jnp.float32)
    out_ref[:, 3:] = jnp.ones((tiles, 1, 8, cols), jnp.float32)

    def pick(i, found):
        picks[found] = i
        return found + (occ_ref[i] != 0).astype(jnp.int32)

    found = lax.fori_loop(0, bricks, pick, 0)

    def pair(step, carry):
        part = step // (tiles // group)
        first_tile = step % (tiles // group) * group
        low = pl.ds(pl.multiple_of(picks[2 * part] * LANES, LANES), LANES)
        high = pl.ds(pl.multiple_of(picks[jnp.minimum(2 * part + 1, found - 1)] * LANES, LANES), LANES)

        def layer(z, states):
            x = jnp.concatenate([feat[z, :, low], feat[z, :, high]], 1)
            lhs = lhs_ref[pl.ds(first_tile, group)].reshape(-1, lhs_ref.shape[2])
            us = jnp.dot(lhs, x, preferred_element_type=jnp.float32)
            fresh = []
            span = us.shape[0] // group // 2
            for t, (colour, remaining) in enumerate(states):
                out = bias_ref[...]
                for p in range(2):
                    at = (2 * t + p) * span
                    u = us[at:at + span]
                    hidden = (u + u * jnp.tanh(u)).astype(jnp.bfloat16)
                    out = out + jnp.dot(mix_ref[p], hidden, preferred_element_type=jnp.float32)
                raw = out[24:32]
                density = jnp.maximum(raw, 0.0) + jnp.log1p(jnp.exp(-jnp.abs(raw)))
                keep = jnp.exp(-optical * density)
                weight = 0.5 * (remaining * (1.0 - keep))
                colour = tuple(
                    colour[i] + (weight + weight * jnp.tanh(out[8 * i:8 * i + 8])) for i in range(3)
                )
                fresh.append((colour, remaining * keep))
            return tuple(fresh)

        zero = jnp.zeros((8, 2 * LANES), jnp.float32)
        states = (((zero, zero, zero), jnp.ones((8, 2 * LANES), jnp.float32)),) * group

        def layer_group(step_z, states):
            for k in range(unroll):
                states = layer(step_z * unroll + k, states)
            return states

        if unroll == layers:
            states = layer_group(0, states)
        else:
            states = lax.fori_loop(0, layers // unroll, layer_group, states)
        for t, (colour, remaining) in enumerate(states):
            for i, value in enumerate(colour + (remaining,)):
                out_ref[first_tile + t, i, :, low] = value[:, :LANES]
                out_ref[first_tile + t, i, :, high] = value[:, LANES:]
        return carry

    lax.fori_loop(0, (found + 1) // 2 * (tiles // group), pair, 0)


def march(volume, above, below, occupancy, w_in, b_in, w_out, b_out, depth_count, optical):
    layers, rows, cols = volume.shape
    channels, hidden = w_in.shape
    tiles = rows // 8
    share = rows // depth_count
    half_in = 0.5 * w_in.astype(jnp.float32)
    rest = 0.5 * b_in
    parts = []
    for unused in range(3):
        part = lax.reduce_precision(rest, 8, 7)
        parts.append(part)
        rest = rest - part
    wide = jnp.repeat(half_in.T, rows, axis=1)
    bias_in = jnp.pad(jnp.stack(parts, 1), ((0, 0), (0, 13)))
    pattern = jnp.concatenate([wide, bias_in], 1)
    scale = jnp.asarray(np.array([0.5, 0.5, 0.5, 1.0], np.float32))
    place = np.zeros((2, 8, 4), np.float32)
    for p in range(2):
        for i in range(4):
            place[p, 4 * p + i, i] = 1.0
    scaled_out = w_out.astype(jnp.float32) * scale[None]
    mix = scaled_out.T[None, :, None, None, :] * jnp.asarray(place)[:, None, :, :, None]
    mix = mix.reshape(2, 32, 4 * hidden).astype(jnp.bfloat16)
    bias = jnp.broadcast_to((b_out * scale)[:, None, None], (4, 8, 2 * LANES)).reshape(32, 2 * LANES)
    vmem = pl.BlockSpec(memory_space=pltpu.VMEM)
    return pl.pallas_call(
        functools.partial(march_kernel, optical, layers, tiles, depth_count),
        out_shape=jax.ShapeDtypeStruct((tiles, 4, 8, cols), jnp.float32),
        in_specs=[pl.BlockSpec(memory_space=pltpu.SMEM)] + [vmem] * 6,
        out_specs=vmem,
        scratch_shapes=[
            pltpu.VMEM((layers, channels * rows + 16, cols), jnp.bfloat16),
            pltpu.VMEM((tiles, 8 * hidden, channels * rows + 16), jnp.bfloat16),
            pltpu.SMEM((occupancy.size + 1,), jnp.int32),
        ],
        compiler_params=pltpu.CompilerParams(vmem_limit_bytes=40 * 1024 * 1024),
        name="march",
    )(occupancy.reshape(-1), volume, above, below, pattern, mix, bias)


def over_pair(front_part, back_part):
    colour = front_part[:3] + front_part[3:4] * back_part[:3]
    remaining = front_part[3:4] * back_part[3:4]
    return jnp.concatenate([colour, remaining], 0)


def shards(volume, occupancy, slab_order, w_in, b_in, w_out, b_out, conv_weight, conv_bias):
    depth_count = lax.axis_size("depth")
    depth_index = lax.axis_index("depth")
    strip_count = lax.axis_size("strip")
    layers, rows_here, columns = volume.shape
    optical = 2.0 / (layers * depth_count)
    down_route = [(i, i + 1) for i in range(strip_count - 1)]
    up_route = [(i + 1, i) for i in range(strip_count - 1)]
    above = lax.ppermute(volume[:, rows_here - 1 :], "strip", down_route)
    below = lax.ppermute(volume[:, :1], "strip", up_route)
    own_order = slab_order[depth_index]
    volume, own_order = lax.optimization_barrier((volume, own_order))
    partial_value = march(
        volume, above, below, occupancy, w_in, b_in, w_out, b_out, depth_count, optical
    )
    rounds = depth_count.bit_length() - 1
    row_share = rows_here // depth_count
    tiles = partial_value.shape[0]
    composed = partial_value.transpose(1, 0, 2, 3)
    for bit_index in range(rounds):
        if composed.shape[1] > 1:
            paired = composed.reshape(4, composed.shape[1] // 2, 2, composed.shape[2], columns)
        else:
            paired = composed.reshape(4, composed.shape[2] // 2 // row_share, 2, row_share, columns)
        mine_bit = jnp.bitwise_and(jnp.right_shift(depth_index, bit_index), 1)
        keep_part = jnp.where(mine_bit == 0, paired[:, :, 0], paired[:, :, 1])
        give_part = jnp.where(mine_bit == 0, paired[:, :, 1], paired[:, :, 0])
        received = partner(give_part, "depth", bit_index)
        in_front = jnp.bitwise_and(jnp.right_shift(own_order, bit_index), 1) == 0
        front_part = jnp.where(in_front, keep_part, received)
        back_part = jnp.where(in_front, received, keep_part)
        composed = over_pair(front_part, back_part)
        if paired.shape[3] == row_share and tiles >> (bit_index + 1) < 1:
            composed = composed.reshape(4, 1, -1, columns)
    composed = composed.reshape(4, row_share, columns)
    picture = composed[:3]
    ring = [(i, (i + 1) % depth_count) for i in range(depth_count)]
    back = [(j, i) for i, j in ring]
    last = depth_count - 1
    corner = [(i * depth_count + last, (i + 1) * depth_count) for i in range(strip_count - 1)]
    corner_back = [(j, i) for i, j in corner]
    from_above = lax.ppermute(picture, "depth", ring)
    from_below = lax.ppermute(picture, "depth", back)
    strip_above = lax.ppermute(picture[:, row_share - 1 :], ("strip", "depth"), corner)
    strip_below = lax.ppermute(picture[:, :1], ("strip", "depth"), corner_back)
    row_above = jnp.where(
        depth_index == 0,
        jnp.concatenate([strip_above, from_above[:, : row_share - 1]], 1),
        from_above,
    )
    row_below = jnp.where(
        depth_index == last,
        jnp.concatenate([from_below[:, 1:], strip_below], 1),
        from_below,
    )
    row_centre = picture
    row_sets = [row_above, row_centre, row_below]
    filtered = jnp.broadcast_to(conv_bias[:, None, None], (3, row_share, columns))
    for row_off in range(3):
        padded = jnp.pad(row_sets[row_off], ((0, 0), (0, 0), (1, 1)))
        for col_off in range(3):
            window = padded[:, :, col_off : col_off + columns]
            filtered = filtered + jnp.sum(
                conv_weight[:, :, row_off, col_off][:, :, None, None] * window[None], axis=1
            )
    return filtered.reshape(3, 1, row_share, 1, columns)


def solution(mesh):
    placed = (
        P("depth", "strip", None),
        P("depth", "strip", None),
        P(),
        P(),
        P(),
        P(),
        P(),
        P(),
        P(),
    )
    return jax.shard_map(
        shards,
        mesh=mesh,
        in_specs=placed,
        out_specs=P(None, "strip", None, "depth", None),
        check_vma=False,
    )
```
